256 devices in a mesh: expert: 64 (over y, z, core), dp: 4 (over x).
Axes of the slice: x: 4, y: 4, z: 8, core: 2. Of those that a mesh axis runs over, the one named last changes fastest.
Arguments:
- tokens: bfloat16 [32768, 512], P(('expert', 'dp')), may hold values from -6 to 6
- routes: int32 [32768, 2], P(('expert', 'dp')), may hold values from 0 to 63, all different within a row; in each aligned block of 128 rows (0 to 127, 128 to 255, ...) at most 16 rows name the same one
- gate_weights: float32 [32768, 2], P(('expert', 'dp')), may hold values from 0.1 to 1
- cotangent: bfloat16 [32768, 512], P(('expert', 'dp')), may hold values from -6 to 6
- expand_weight: bfloat16 [64, 512, 2048], P('expert'), may hold values from -0.25 to 0.25
- reduce_weight: bfloat16 [64, 2048, 512], P('expert'), may hold values from -0.125 to 0.125
Outputs:
- layer_out: bfloat16 [32768, 512], P(('expert', 'dp'))
- token_grad: bfloat16 [32768, 512], P(('expert', 'dp'))
- gate_grad: float32 [32768, 2], P(('expert', 'dp'))
- expand_grad: float32 [64, 512, 2048], P('expert', 'dp')
- reduce_grad: float32 [64, 2048, 512], P('expert', None, 'dp')
The draws below stay inside these ranges and needn't reach their ends.
Inputs may be any that keep to these rules, and one draw needn't show every extreme that they name: `routes`: the two experts of a token differ. Within the 128 rows of one device no expert is named by more than 16 rows, a bound that some block reaches; every expert is named by some row.
All inputs are finite; a program needn't handle non-finite values.
Results may differ from the reference program's by a relative error of at most 0.0085.
Values may be sent and summed in bfloat16 or wider, within the bound.
No kernel may reach another device: no remote copies, remote signals or barrier semaphores. Data moves between devices by JAX's collectives and lax.ppermute only.
A program may use at most 64 MiB of HBM per device.

```python
import math
import jax
import jax.numpy as jnp
import numpy as np
from jax import lax

D = 512
H = 2048
TOK_DEV = 128
EXPERTS = 64
CAP = 16
TOKENS = 32768
N_EXPERT = 64
N_DP = 4


def shard_levels(key, extent, shards, low, largest):
    loudness, own = 1.0, jax.random.fold_in(key, 6)
    for position, shards_of in shards:
        heights = jnp.exp(jax.random.uniform(jax.random.fold_in(own, position), (shards_of,), jnp.float32, low / len(shards), largest / len(shards)))
        loudness = loudness * jnp.repeat(heights, extent[position] // shards_of).reshape([-1 if axis == position else 1 for axis in range(len(extent))])
    return loudness


def deal_out(rng, own, number, rows, count, top, bound, lean):
    sequence = jax.random.permutation(rng, count)
    crowded, usual = load_shares(count, rows * top, bound, lean, True), load_shares(count, rows * top, bound, lean, False)
    places = jnp.arange(count)

    def named(lengths, rotation):
        used = int((lengths > 0).sum())
        fixed = max(1, used // 4)
        moved = fixed + (places - fixed + rotation * (used - fixed)) % max(1, count - fixed)
        return jnp.zeros((count,), jnp.int32).at[sequence[jnp.where(places < fixed, places, moved)]].set(jnp.asarray(lengths, jnp.int32))

    lengths = jnp.where(number % 4 == 0, named(crowded, number // 4), named(usual, number - number // 4 - 1))
    mixed = jax.random.permutation(jax.random.fold_in(own, 3), count)
    source_of, taker = mixed[0:count // 2 * 2:2], mixed[1:count // 2 * 2:2]
    slack = jnp.minimum(lengths[source_of] - 1, bound - lengths[taker]) // 2
    slack = jnp.where((source_of == sequence[0]) | (taker == sequence[0]) | (lengths[taker] == 0), 0, jnp.maximum(slack, 0))
    moved = jax.random.randint(jax.random.fold_in(own, 4), (count // 2,), 0, 1 << 20) % (slack + 1)
    lengths = lengths.at[source_of].add(-moved).at[taker].add(moved)
    members = jnp.searchsorted(jnp.cumsum(lengths), jnp.arange(rows * top), side="right").astype(jnp.int32)
    table = members.reshape(top, rows).T
    table = table[jax.random.permutation(jax.random.fold_in(own, 1), rows)]
    rotation = jax.random.randint(jax.random.fold_in(own, 2), (rows, 1), 0, top)
    return jnp.take_along_axis(table, (jnp.arange(top)[None, :] + rotation) % top, axis=1)


def load_shares(number_of, total, limit, lean, full):
    loads = [(1 << 20) // math.isqrt(standing ** lean) + 1 for standing in range(1, number_of + 1)]
    largest = limit if full else min(limit, max(-(-total // number_of), total * loads[0] // sum(loads)))
    least = 1 if total - largest >= number_of - 1 else 0
    counts, rest = [largest] + [least] * (number_of - 1), total - largest - least * (number_of - 1)
    while rest > 0:
        movable = [i for i in range(1, number_of) if counts[i] < largest] or [i for i in range(1, number_of) if counts[i] < limit]
        pool, budget = sum([loads[i] for i in movable]), rest
        for i in movable:
            addition = min(limit - counts[i], max(1, budget * loads[i] // pool), rest)
            counts[i] = counts[i] + addition
            rest = rest - addition
    return np.array(counts)


def normal_values(key, dims, spread, reach, cuts=(), kind=jnp.bfloat16):
    entries = jax.random.normal(key, dims, jnp.float32) * spread
    if len(cuts) > 0:
        entries = shard_levels(key, dims, cuts, -0.22, 0.18) * entries
    return jnp.clip(entries, min=-reach, max=reach).astype(kind)


def setup_inputs(seed: int = 0) -> dict:
    key_of = jax.random.split(jax.random.key(seed), 7)
    tokens = normal_values(key_of[0], (TOKENS, D), 1.0, 6.0, ((0, 256),))
    routes_keys = jax.random.split(jax.random.fold_in(key_of[1], 1), TOKENS // TOK_DEV)
    routes_turns = jax.random.permutation(jax.random.fold_in(key_of[1], 3), TOKENS // TOK_DEV)
    routes = jax.vmap(lambda own, number: deal_out(jax.random.fold_in(key_of[1], 2), own, number, TOK_DEV, EXPERTS, 2, CAP, 2))(routes_keys, routes_turns).reshape((TOKENS, 2))
    gate_weights = jnp.clip(0.1 + 0.9 * jax.random.uniform(key_of[2], (TOKENS, 2), jnp.float32) ** shard_levels(key_of[2], (TOKENS, 2), ((0, 256),), -0.2, 0.2), 0.1, 1.0)
    cotangent = normal_values(key_of[3], (TOKENS, D), 1.0, 6.0, ((0, 256),))
    expand_weight = normal_values(key_of[4], (EXPERTS, D, H), D ** -0.5, 0.25, ((0, 64),))
    reduce_weight = normal_values(key_of[5], (EXPERTS, H, D), H ** -0.5, 0.125, ((0, 64),))
    return {"tokens": tokens, "routes": routes, "gate_weights": gate_weights, "cotangent": cotangent, "expand_weight": expand_weight, "reduce_weight": reduce_weight}


tanh_scale = math.sqrt(2.0 / math.pi)
cubic_term = 0.044715

def activate(inputs):
    argument = tanh_scale * (inputs + cubic_term * inputs * inputs * inputs)
    return 0.5 * inputs * (1.0 + jnp.tanh(argument))

def activate_slope(inputs):
    argument = tanh_scale * (inputs + cubic_term * inputs * inputs * inputs)
    tangent = jnp.tanh(argument)
    return 0.5 * (1.0 + tangent) + 0.5 * inputs * (1.0 - tangent * tangent) * tanh_scale * (1.0 + 3.0 * cubic_term * inputs * inputs)

def slot_positions(route_ids, experts):
    onehot = (route_ids[..., None] == jnp.arange(experts, dtype=jnp.int32)).astype(jnp.int32)
    counted = jnp.cumsum(onehot, axis=-2)
    return (lax.optimization_barrier(jnp.sum(counted * onehot, axis=-1)) - 1).astype(jnp.int32)

def reference(tokens, routes, gate_weights, cotangent, expand_weight, reduce_weight):
    devices = N_EXPERT * N_DP
    route_ids = routes.reshape(devices, TOK_DEV * 2)
    slot_index = slot_positions(route_ids, EXPERTS).reshape(-1)
    route_flat = route_ids.reshape(-1).astype(jnp.int32)
    device_ids = jnp.repeat(jnp.arange(devices, dtype=jnp.int32), TOK_DEV * 2)
    source_ids = device_ids // N_DP
    replica_ids = device_ids % N_DP
    token_rows = jnp.repeat(tokens, 2, axis=0)
    scaled = (gate_weights.astype(jnp.float32)[:, :, None] * cotangent.astype(jnp.float32)[:, None, :]).astype(jnp.bfloat16).reshape(TOKENS * 2, D)
    buffer_shape = (EXPERTS, N_DP, N_EXPERT, CAP, D)
    sent_rows = jnp.zeros(buffer_shape, jnp.bfloat16).at[route_flat, replica_ids, source_ids, slot_index].set(token_rows)
    sent_grads = jnp.zeros(buffer_shape, jnp.bfloat16).at[route_flat, replica_ids, source_ids, slot_index].set(scaled)

    def per_expert(operands):
        sent_block, grad_block, expand_local, reduce_local = operands
        flat_rows = sent_block.reshape(N_DP * N_EXPERT * CAP, D)
        flat_grads = grad_block.reshape(N_DP * N_EXPERT * CAP, D)
        projected = jnp.dot(flat_rows, expand_local, preferred_element_type=jnp.float32)
        hidden = activate(projected).astype(jnp.bfloat16)
        expert_out = jnp.dot(hidden, reduce_local, preferred_element_type=jnp.float32).astype(jnp.bfloat16)
        hidden_grad = jnp.dot(flat_grads, reduce_local.T, preferred_element_type=jnp.float32)
        projected_grad = (hidden_grad * activate_slope(projected)).astype(jnp.bfloat16)
        input_grad = jnp.dot(projected_grad, expand_local.T, preferred_element_type=jnp.float32).astype(jnp.bfloat16)
        outer_partial = jnp.einsum('prh,prd->phd', hidden.reshape(N_DP, -1, H).astype(jnp.float32), flat_grads.reshape(N_DP, -1, D).astype(jnp.float32))
        inner_partial = jnp.einsum('prd,prh->pdh', flat_rows.reshape(N_DP, -1, D).astype(jnp.float32), projected_grad.reshape(N_DP, -1, H).astype(jnp.float32))
        outer_partial = lax.optimization_barrier(outer_partial.astype(jnp.bfloat16)).astype(jnp.float32)
        inner_partial = lax.optimization_barrier(inner_partial.astype(jnp.bfloat16)).astype(jnp.float32)
        return (expert_out.reshape(N_DP, N_EXPERT, CAP, D), input_grad.reshape(N_DP, N_EXPERT, CAP, D), lax.optimization_barrier(jnp.sum(inner_partial, axis=0)), lax.optimization_barrier(jnp.sum(outer_partial, axis=0)))
    returned_out, returned_grad, expand_grad, reduce_grad = lax.map(per_expert, (sent_rows, sent_grads, expand_weight, reduce_weight))
    slot_out = returned_out[route_flat, replica_ids, source_ids, slot_index].reshape(TOKENS, 2, D).astype(jnp.float32)
    slot_grad = returned_grad[route_flat, replica_ids, source_ids, slot_index].reshape(TOKENS, 2, D).astype(jnp.float32)
    layer_out = lax.optimization_barrier(jnp.sum(gate_weights.astype(jnp.float32)[:, :, None] * slot_out, axis=1)).astype(jnp.bfloat16)
    gate_grad = lax.optimization_barrier(jnp.sum(cotangent.astype(jnp.float32)[:, None, :] * slot_out, axis=2))
    token_grad = lax.optimization_barrier(jnp.sum(slot_grad, axis=1)).astype(jnp.bfloat16)
    return (layer_out, token_grad, gate_grad, expand_grad, reduce_grad)
```

```python
import functools
import math

import jax
import jax.numpy as jnp
from jax import lax
from jax.experimental import pallas as pl
from jax.experimental.pallas import tpu as pltpu
from jax.sharding import PartitionSpec as P

tanh_scale = math.sqrt(2.0 / math.pi)
cubic_term = 0.044715

F32 = jnp.float32
BF16 = jnp.bfloat16
NT = (((1,), (1,)), ((), ()))
VMEM_LIMIT = 60 * 1024 * 1024


def iota(shape, axis):
    return lax.broadcasted_iota(jnp.int32, shape, axis)


def column(row):
    n = row.shape[1]
    eye = iota((n, n), 0) == iota((n, n), 1)
    return jnp.sum(jnp.where(eye, row, jnp.zeros_like(row)), axis=1, keepdims=True)


def as_row(col):
    n = col.shape[0]
    eye = iota((n, n), 0) == iota((n, n), 1)
    return jnp.sum(jnp.where(eye, col, jnp.zeros_like(col)), axis=0, keepdims=True)


def destinations(routes_ref, experts, capacity):
    tok = routes_ref.shape[1]
    first, second = routes_ref[0:1, :], routes_ref[1:2, :]
    ids = iota((experts, tok), 0)
    hot0 = (ids == first).astype(F32)
    hot1 = (ids == second).astype(F32)
    before = (iota((tok, tok), 0) < iota((tok, tok), 1)).astype(F32).astype(BF16)
    count0 = jnp.dot(hot0.astype(BF16), before, preferred_element_type=F32)
    count1 = jnp.dot(hot1.astype(BF16), before, preferred_element_type=F32)
    count1 = count1 + jnp.sum(hot0, axis=1, keepdims=True)
    pos0 = jnp.sum(hot0 * count0, axis=0, keepdims=True)
    pos1 = jnp.sum(hot1 * count1, axis=0, keepdims=True)
    return (
        first * capacity + pos0.astype(jnp.int32),
        second * capacity + pos1.astype(jnp.int32),
    )


def pack_kernel(experts, capacity, routes_ref, gates_ref, tokens_ref, cot_ref, out_ref):
    slots = experts * capacity
    tok, width = tokens_ref.shape
    dest0, dest1 = destinations(routes_ref, experts, capacity)
    rows = iota((slots, tok), 0)
    pick = jnp.concatenate(
        [(rows == dest0).astype(F32).astype(BF16), (rows == dest1).astype(F32).astype(BF16)],
        axis=1,
    )
    cot = cot_ref[...].astype(F32)
    grad0 = (column(gates_ref[0:1, :]) * cot).astype(BF16)
    grad1 = (column(gates_ref[1:2, :]) * cot).astype(BF16)
    tokens = tokens_ref[...]
    out_ref[:, :width] = jnp.dot(
        pick, jnp.concatenate([tokens, tokens], axis=0), preferred_element_type=F32
    ).astype(BF16)
    out_ref[:, width:] = jnp.dot(
        pick, jnp.concatenate([grad0, grad1], axis=0), preferred_element_type=F32
    ).astype(BF16)


def combine_kernel(
    experts, capacity, routes_ref, gates_ref, cot_ref, ret_ref, out_ref, tgrad_ref, ggrad_ref
):
    slots = experts * capacity
    tok, width = cot_ref.shape
    dest0, dest1 = destinations(routes_ref, experts, capacity)
    cols = iota((tok, slots), 1)
    dest0 = column(dest0.astype(F32)).astype(jnp.int32)
    dest1 = column(dest1.astype(F32)).astype(jnp.int32)
    pick = jnp.concatenate(
        [(cols == dest0).astype(F32).astype(BF16), (cols == dest1).astype(F32).astype(BF16)],
        axis=0,
    )
    slot_out = jnp.dot(pick, ret_ref[:, :width], preferred_element_type=F32)
    slot_grad = jnp.dot(pick, ret_ref[:, width:], preferred_element_type=F32)
    out0, out1 = slot_out[:tok], slot_out[tok:]
    gate0, gate1 = column(gates_ref[0:1, :]), column(gates_ref[1:2, :])
    out_ref[...] = (gate0 * out0 + gate1 * out1).astype(BF16)
    tgrad_ref[...] = (slot_grad[:tok] + slot_grad[tok:]).astype(BF16)
    cot = cot_ref[...].astype(F32)
    ggrad_ref[0:1, :] = as_row(jnp.sum(cot * out0, axis=1, keepdims=True))
    ggrad_ref[1:2, :] = as_row(jnp.sum(cot * out1, axis=1, keepdims=True))


def expert_kernel(chunk, rows_ref, w1_ref, w2_ref, ret_ref, hidden_ref, pgrad_ref):
    width = w1_ref.shape[0]
    inner = w1_ref.shape[1]
    x = rows_ref[:, :width]
    g = rows_ref[:, width:]
    for start in range(0, inner, chunk):
        part = slice(start, start + chunk)
        v = jnp.dot(x, w1_ref[:, part], preferred_element_type=F32)
        hgrad = lax.dot_general(g, w2_ref[part, :], NT, preferred_element_type=F32)
        sq = v * v
        half = 0.5 + 0.5 * jnp.tanh(v * (tanh_scale + (tanh_scale * cubic_term) * sq))
        hidden = v * half
        slope = half + hidden * (1.0 - half) * (
            2.0 * tanh_scale + (6.0 * tanh_scale * cubic_term) * sq
        )
        hidden_ref[:, part] = hidden.astype(BF16)
        pgrad_ref[:, part] = (hgrad * slope).astype(BF16)
    ret_ref[:, :width] = jnp.dot(
        hidden_ref[...], w2_ref[...], preferred_element_type=F32
    ).astype(BF16)
    ret_ref[:, width:] = lax.dot_general(
        pgrad_ref[...], w1_ref[...], NT, preferred_element_type=F32
    ).astype(BF16)


def weight_kernel(n, place_ref, *refs):
    xs, gs = refs[:n], refs[n : 2 * n]
    hidden_ref, pgrad_ref = refs[2 * n : 2 * n + 2]
    outs = refs[2 * n + 2 : 3 * n + 2]
    xt_ref, gt_ref = refs[3 * n + 2 :]
    part = xs[0].shape[1]

    @pl.when(pl.program_id(0) == 0)
    def _():
        for d in range(n):
            xt_ref[d * part : (d + 1) * part, :] = xs[d][...].T
            gt_ref[d * part : (d + 1) * part, :] = gs[d][...].T

    inner = jnp.dot(xt_ref[...], pgrad_ref[...], preferred_element_type=F32).astype(BF16)
    outer = jnp.dot(gt_ref[...], hidden_ref[...], preferred_element_type=F32).astype(BF16)
    for d in range(n):
        outs[d][0] = inner[d * part : (d + 1) * part]
        outs[d][1] = outer[d * part : (d + 1) * part]


def sum_kernel(n, *refs):
    expand_ref, reduce_ref = refs[n:]
    expand = refs[0][0].astype(F32)
    reduce = refs[0][1].astype(F32)
    for d in range(1, n):
        expand = expand + refs[d][0].astype(F32)
        reduce = reduce + refs[d][1].astype(F32)
    expand_ref[...] = expand
    reduce_ref[...] = reduce.T


def params():
    return pltpu.CompilerParams(vmem_limit_bytes=VMEM_LIMIT)


def shards(tokens, routes, gate_weights, cotangent, expand_weight, reduce_weight):
    tok, width = tokens.shape
    experts = lax.axis_size("expert")
    n_dp = lax.axis_size("dp")
    capacity = 8 * tok // experts
    slots = experts * capacity
    w1, w2 = expand_weight[0], reduce_weight[0]
    inner = w1.shape[1]
    routes_t, gates_t = routes.T, gate_weights.T
    part = width // n_dp

    packed = pl.pallas_call(
        functools.partial(pack_kernel, experts, capacity),
        out_shape=jax.ShapeDtypeStruct((slots, 2 * width), BF16),
        compiler_params=params(),
        name="pack",
    )(routes_t, gates_t, tokens, cotangent)
    arrived = lax.all_to_all(
        packed.reshape(experts, capacity, 2 * width), "expert", 0, 0, tiled=True
    ).reshape(slots, 2 * width)

    tile = 256
    once = pl.Buffered(1)
    ret, hidden, pgrad = pl.pallas_call(
        functools.partial(expert_kernel, 512),
        grid=(slots // tile,),
        in_specs=[
            pl.BlockSpec((tile, 2 * width), lambda i: (i, 0)),
            pl.BlockSpec((width, inner), lambda i: (0, 0), pipeline_mode=once),
            pl.BlockSpec((inner, width), lambda i: (0, 0), pipeline_mode=once),
        ],
        out_specs=[
            pl.BlockSpec((tile, 2 * width), lambda i: (i, 0)),
            pl.BlockSpec((tile, inner), lambda i: (i, 0)),
            pl.BlockSpec((tile, inner), lambda i: (i, 0)),
        ],
        out_shape=[
            jax.ShapeDtypeStruct((slots, 2 * width), BF16),
            jax.ShapeDtypeStruct((slots, inner), BF16),
            jax.ShapeDtypeStruct((slots, inner), BF16),
        ],
        compiler_params=params(),
        cost_estimate=pl.CostEstimate(
            flops=8 * slots * width * inner, bytes_accessed=16 << 20, transcendentals=0
        ),
        name="expert",
    )(arrived, w1, w2)
    returned = lax.all_to_all(
        ret.reshape(experts, capacity, 2 * width), "expert", 0, 0, tiled=True
    ).reshape(slots, 2 * width)

    place = lax.axis_index("dp").astype(jnp.int32).reshape(1)
    htile = 512

    def piece(d, base):
        return pl.BlockSpec(
            (slots, part),
            lambda i, p: (0, base + lax.rem(p[0] + d, n_dp)),
            pipeline_mode=once,
        )

    pieces = pl.pallas_call(
        functools.partial(weight_kernel, n_dp),
        grid_spec=pltpu.PrefetchScalarGridSpec(
            num_scalar_prefetch=1,
            grid=(inner // htile,),
            in_specs=[piece(d, 0) for d in range(n_dp)]
            + [piece(d, n_dp) for d in range(n_dp)]
            + [pl.BlockSpec((slots, htile), lambda i, p: (0, i))] * 2,
            out_specs=[pl.BlockSpec((2, part, htile), lambda i, p: (0, 0, i))] * n_dp,
            scratch_shapes=[pltpu.VMEM((width, slots), BF16)] * 2,
        ),
        out_shape=[jax.ShapeDtypeStruct((2, part, inner), BF16)] * n_dp,
        compiler_params=params(),
        cost_estimate=pl.CostEstimate(
            flops=4 * slots * width * inner, bytes_accessed=14 << 20, transcendentals=0
        ),
        name="weights",
    )(place, *([arrived] * (2 * n_dp)), hidden, pgrad)
    landed = [pieces[0]] + [
        lax.ppermute(pieces[d], "dp", [(i, (i + d) % n_dp) for i in range(n_dp)])
        for d in range(1, n_dp)
    ]
    expand_grad, reduce_grad = pl.pallas_call(
        functools.partial(sum_kernel, n_dp),
        grid=(inner // htile,),
        in_specs=[pl.BlockSpec((2, part, htile), lambda i: (0, 0, i))] * n_dp,
        out_specs=[
            pl.BlockSpec((part, htile), lambda i: (0, i)),
            pl.BlockSpec((htile, part), lambda i: (i, 0)),
        ],
        out_shape=[
            jax.ShapeDtypeStruct((part, inner), F32),
            jax.ShapeDtypeStruct((inner, part), F32),
        ],
        compiler_params=params(),
        name="total",
    )(*landed)

    layer_out, token_grad, gate_grad = pl.pallas_call(
        functools.partial(combine_kernel, experts, capacity),
        out_shape=[
            jax.ShapeDtypeStruct((tok, width), BF16),
            jax.ShapeDtypeStruct((tok, width), BF16),
            jax.ShapeDtypeStruct((2, tok), F32),
        ],
        compiler_params=params(),
        name="combine",
    )(routes_t, gates_t, cotangent, returned)
    return (layer_out, token_grad, gate_grad.T, expand_grad[None], reduce_grad[None])


def solution(mesh):
    return jax.shard_map(
        shards,
        mesh=mesh,
        in_specs=(
            P(("expert", "dp"), None),
            P(("expert", "dp"), None),
            P(("expert", "dp"), None),
            P(("expert", "dp"), None),
            P("expert", None, None),
            P("expert", None, None),
        ),
        out_specs=(
            P(("expert", "dp"), None),
            P(("expert", "dp"), None),
            P(("expert", "dp"), None),
            P("expert", "dp", None),
            P("expert", None, "dp"),
        ),
        check_vma=False,
    )
```

```python
import functools
import math

import jax
import jax.numpy as jnp
from jax import lax
from jax.experimental import pallas as pl
from jax.experimental.pallas import tpu as pltpu
from jax.sharding import PartitionSpec as P


tanh_scale = math.sqrt(2.0 / math.pi)
cubic_term = 0.044715

F32 = jnp.float32
BF16 = jnp.bfloat16
NT = (((1,), (1,)), ((), ()))
VMEM_LIMIT = 60 * 1024 * 1024


def iota(shape, axis):
    return lax.broadcasted_iota(jnp.int32, shape, axis)


def column(row):
    n = row.shape[1]
    eye = iota((n, n), 0) == iota((n, n), 1)
    return jnp.sum(jnp.where(eye, row, jnp.zeros_like(row)), axis=1, keepdims=True)


def as_row(col):
    n = col.shape[0]
    eye = iota((n, n), 0) == iota((n, n), 1)
    return jnp.sum(jnp.where(eye, col, jnp.zeros_like(col)), axis=0, keepdims=True)


def destinations(routes_ref, experts, capacity):
    tok = routes_ref.shape[1]
    first, second = routes_ref[0:1, :], routes_ref[1:2, :]
    ids = iota((experts, tok), 0)
    hot0 = (ids == first).astype(F32)
    hot1 = (ids == second).astype(F32)
    before = (iota((tok, tok), 0) < iota((tok, tok), 1)).astype(F32).astype(BF16)
    count0 = jnp.dot(hot0.astype(BF16), before, preferred_element_type=F32)
    count1 = jnp.dot(hot1.astype(BF16), before, preferred_element_type=F32)
    count1 = count1 + jnp.sum(hot0, axis=1, keepdims=True)
    pos0 = jnp.sum(hot0 * count0, axis=0, keepdims=True)
    pos1 = jnp.sum(hot1 * count1, axis=0, keepdims=True)
    return (
        first * capacity + pos0.astype(jnp.int32),
        second * capacity + pos1.astype(jnp.int32),
    )


def pick_rows(experts, capacity, routes_ref):
    dest0, dest1 = destinations(routes_ref, experts, capacity)
    rows = iota((experts * capacity, routes_ref.shape[1]), 0)
    return (
        (rows == dest0).astype(F32).astype(BF16),
        (rows == dest1).astype(F32).astype(BF16),
    )


def pick_cols(experts, capacity, routes_ref):
    dest0, dest1 = destinations(routes_ref, experts, capacity)
    cols = iota((routes_ref.shape[1], experts * capacity), 1)
    dest0 = column(dest0.astype(F32)).astype(jnp.int32)
    dest1 = column(dest1.astype(F32)).astype(jnp.int32)
    return (
        (cols == dest0).astype(F32).astype(BF16),
        (cols == dest1).astype(F32).astype(BF16),
    )


def pack_tokens_kernel(experts, capacity, routes_ref, tokens_ref, out_ref):
    pick0, pick1 = pick_rows(experts, capacity, routes_ref)
    out_ref[...] = jnp.dot(
        pick0 + pick1, tokens_ref[...], preferred_element_type=F32
    ).astype(BF16)


def pack_grads_kernel(experts, capacity, routes_ref, gates_ref, cot_ref, out_ref):
    pick = jnp.concatenate(pick_rows(experts, capacity, routes_ref), axis=1)
    cot = cot_ref[...].astype(F32)
    grad0 = (column(gates_ref[0:1, :]) * cot).astype(BF16)
    grad1 = (column(gates_ref[1:2, :]) * cot).astype(BF16)
    out_ref[...] = jnp.dot(
        pick, jnp.concatenate([grad0, grad1], axis=0), preferred_element_type=F32
    ).astype(BF16)


def output_kernel(experts, capacity, routes_ref, gates_ref, cot_ref, ret_ref, out_ref, ggrad_ref):
    tok = cot_ref.shape[0]
    pick = jnp.concatenate(pick_cols(experts, capacity, routes_ref), axis=0)
    slot_out = jnp.dot(pick, ret_ref[...], preferred_element_type=F32)
    out0, out1 = slot_out[:tok], slot_out[tok:]
    gate0, gate1 = column(gates_ref[0:1, :]), column(gates_ref[1:2, :])
    out_ref[...] = (gate0 * out0 + gate1 * out1).astype(BF16)
    cot = cot_ref[...].astype(F32)
    ggrad_ref[0:1, :] = as_row(jnp.sum(cot * out0, axis=1, keepdims=True))
    ggrad_ref[1:2, :] = as_row(jnp.sum(cot * out1, axis=1, keepdims=True))


def tgrad_kernel(experts, capacity, routes_ref, ret_ref, tgrad_ref):
    pick0, pick1 = pick_cols(experts, capacity, routes_ref)
    tgrad_ref[...] = jnp.dot(
        pick0 + pick1, ret_ref[...], preferred_element_type=F32
    ).astype(BF16)


def forward_kernel(chunk, x_ref, w1_ref, w2_ref, out_ref, hidden_ref, slope_ref):
    x = x_ref[...]
    for start in range(0, w1_ref.shape[1], chunk):
        part = slice(start, start + chunk)
        v = jnp.dot(x, w1_ref[:, part], preferred_element_type=F32)
        sq = v * v
        half = 0.5 + 0.5 * jnp.tanh(v * (tanh_scale + (tanh_scale * cubic_term) * sq))
        hidden = v * half
        slope = half + hidden * (1.0 - half) * (
            2.0 * tanh_scale + (6.0 * tanh_scale * cubic_term) * sq
        )
        hidden_ref[:, part] = hidden.astype(BF16)
        slope_ref[:, part] = slope.astype(BF16)
    out_ref[...] = jnp.dot(
        hidden_ref[...], w2_ref[...], preferred_element_type=F32
    ).astype(BF16)


def backward_kernel(chunk, g_ref, slope_ref, w1_ref, w2_ref, ig_ref, pgrad_ref):
    g = g_ref[...]
    for start in range(0, w1_ref.shape[1], chunk):
        part = slice(start, start + chunk)
        hgrad = lax.dot_general(g, w2_ref[part, :], NT, preferred_element_type=F32)
        pgrad_ref[:, part] = (hgrad * slope_ref[:, part].astype(F32)).astype(BF16)
    ig_ref[...] = lax.dot_general(
        pgrad_ref[...], w1_ref[...], NT, preferred_element_type=F32
    ).astype(BF16)


def weight_kernel(n, place_ref, *refs):
    pieces, right_ref = refs[:n], refs[n]
    outs = refs[n + 1 : 2 * n + 1]
    left_ref = refs[2 * n + 1]
    part = pieces[0].shape[1]

    @pl.when(pl.program_id(0) == 0)
    def _():
        for d in range(n):
            left_ref[d * part : (d + 1) * part, :] = pieces[d][...].T

    product = jnp.dot(left_ref[...], right_ref[...], preferred_element_type=F32).astype(BF16)
    for d in range(n):
        outs[d][...] = product[d * part : (d + 1) * part]


def sum_kernel(n, *refs):
    expand_ref, reduce_ref = refs[2 * n :]
    expand = refs[0][...].astype(F32)
    reduce = refs[n][...].astype(F32)
    for d in range(1, n):
        expand = expand + refs[d][...].astype(F32)
        reduce = reduce + refs[n + d][...].astype(F32)
    expand_ref[...] = expand
    reduce_ref[...] = reduce.T


def params():
    return pltpu.CompilerParams(vmem_limit_bytes=VMEM_LIMIT)


def cost(flops, moved):
    return pl.CostEstimate(flops=flops, bytes_accessed=moved, transcendentals=0)


def shards(tokens, routes, gate_weights, cotangent, expand_weight, reduce_weight):
    tok, width = tokens.shape
    experts = lax.axis_size("expert")
    n_dp = lax.axis_size("dp")
    capacity = 8 * tok // experts
    slots = experts * capacity
    w1, w2 = expand_weight[0], reduce_weight[0]
    inner = w1.shape[1]
    routes_t, gates_t = routes.T, gate_weights.T
    part = width // n_dp
    matmul = 2 * slots * width * inner
    mib = 1 << 20
    once = pl.Buffered(1)
    tile, htile = 256, 512
    rows = jax.ShapeDtypeStruct((slots, width), BF16)
    wide = jax.ShapeDtypeStruct((slots, inner), BF16)

    def exchange(x):
        return lax.all_to_all(
            x.reshape(experts, capacity, width), "expert", 0, 0, tiled=True
        ).reshape(slots, width)

    def row_spec(n):
        return pl.BlockSpec((tile, n), lambda i: (i, 0))

    weight_specs = [
        pl.BlockSpec((width, inner), lambda i: (0, 0), pipeline_mode=once),
        pl.BlockSpec((inner, width), lambda i: (0, 0), pipeline_mode=once),
    ]

    send_tok = pl.pallas_call(
        functools.partial(pack_tokens_kernel, experts, capacity),
        out_shape=rows,
        compiler_params=params(),
        cost_estimate=cost(2 * slots * tok * width, mib),
        name="pack_tokens",
    )(routes_t, tokens)
    x = exchange(send_tok)
    send_grad = pl.pallas_call(
        functools.partial(pack_grads_kernel, experts, capacity),
        out_shape=rows,
        compiler_params=params(),
        cost_estimate=cost(4 * slots * tok * width, mib),
        name="pack_grads",
    )(routes_t, gates_t, cotangent)
    g = exchange(send_grad)
    out, hidden, slope = pl.pallas_call(
        functools.partial(forward_kernel, 512),
        grid=(slots // tile,),
        in_specs=[row_spec(width)] + weight_specs,
        out_specs=[row_spec(width), row_spec(inner), row_spec(inner)],
        out_shape=[rows, wide, wide],
        compiler_params=params(),
        cost_estimate=cost(2 * matmul, 14 * mib),
        name="forward",
    )(x, w1, w2)
    out_back = exchange(out)
    place = lax.axis_index("dp").astype(jnp.int32).reshape(1)

    def piece(d):
        return pl.BlockSpec(
            (slots, part),
            lambda i, p: (0, lax.rem(p[0] + d, n_dp)),
            pipeline_mode=once,
        )

    def weight_grad(left, right):
        pieces = pl.pallas_call(
            functools.partial(weight_kernel, n_dp),
            grid_spec=pltpu.PrefetchScalarGridSpec(
                num_scalar_prefetch=1,
                grid=(inner // htile,),
                in_specs=[piece(d) for d in range(n_dp)]
                + [pl.BlockSpec((slots, htile), lambda i, p: (0, i))],
                out_specs=[pl.BlockSpec((part, htile), lambda i, p: (0, i))] * n_dp,
                scratch_shapes=[pltpu.VMEM((width, slots), BF16)],
            ),
            out_shape=[jax.ShapeDtypeStruct((part, inner), BF16)] * n_dp,
            compiler_params=params(),
            cost_estimate=cost(matmul, 7 * mib),
        )(place, *([left] * n_dp), right)
        return [pieces[0]] + [
            lax.ppermute(pieces[d], "dp", [(i, (i + d) % n_dp) for i in range(n_dp)])
            for d in range(1, n_dp)
        ]

    reduce_parts = weight_grad(g, hidden)
    igrad, pgrad = pl.pallas_call(
        functools.partial(backward_kernel, 512),
        grid=(slots // tile,),
        in_specs=[row_spec(width), row_spec(inner)] + weight_specs,
        out_specs=[row_spec(width), row_spec(inner)],
        out_shape=[rows, wide],
        compiler_params=params(),
        cost_estimate=cost(2 * matmul, 14 * mib),
        name="backward",
    )(g, slope, w1, w2)
    ig_back = exchange(igrad)
    expand_parts = weight_grad(x, pgrad)
    layer_out, gate_grad = pl.pallas_call(
        functools.partial(output_kernel, experts, capacity),
        out_shape=[
            jax.ShapeDtypeStruct((tok, width), BF16),
            jax.ShapeDtypeStruct((2, tok), F32),
        ],
        compiler_params=params(),
        cost_estimate=cost(4 * slots * tok * width, 2 * mib),
        name="output",
    )(routes_t, gates_t, cotangent, out_back)
    expand_grad, reduce_grad = pl.pallas_call(
        functools.partial(sum_kernel, n_dp),
        grid=(inner // htile,),
        in_specs=[pl.BlockSpec((part, htile), lambda i: (0, i))] * (2 * n_dp),
        out_specs=[
            pl.BlockSpec((part, htile), lambda i: (0, i)),
            pl.BlockSpec((htile, part), lambda i: (i, 0)),
        ],
        out_shape=[
            jax.ShapeDtypeStruct((part, inner), F32),
            jax.ShapeDtypeStruct((inner, part), F32),
        ],
        compiler_params=params(),
        cost_estimate=cost(mib, 6 * mib),
        name="total",
    )(*expand_parts, *reduce_parts)
    token_grad = pl.pallas_call(
        functools.partial(tgrad_kernel, experts, capacity),
        out_shape=jax.ShapeDtypeStruct((tok, width), BF16),
        compiler_params=params(),
        cost_estimate=cost(2 * slots * tok * width, mib),
        name="token_grad",
    )(routes_t, ig_back)
    return (layer_out, token_grad, gate_grad.T, expand_grad[None], reduce_grad[None])


def solution(mesh):
    return jax.shard_map(
        shards,
        mesh=mesh,
        in_specs=(
            P(("expert", "dp"), None),
            P(("expert", "dp"), None),
            P(("expert", "dp"), None),
            P(("expert", "dp"), None),
            P("expert", None, None),
            P("expert", None, None),
        ),
        out_specs=(
            P(("expert", "dp"), None),
            P(("expert", "dp"), None),
            P(("expert", "dp"), None),
            P("expert", "dp", None),
            P("expert", None, "dp"),
        ),
        check_vma=False,
    )
```

```python
import functools
import math

import jax
import jax.numpy as jnp
from jax import lax
from jax.experimental import pallas as pl
from jax.experimental.pallas import tpu as pltpu
from jax.sharding import PartitionSpec as P


tanh_scale = math.sqrt(2.0 / math.pi)
cubic_term = 0.044715

F32 = jnp.float32
BF16 = jnp.bfloat16
NT = (((1,), (1,)), ((), ()))
VMEM_LIMIT = 54 * 1024 * 1024


def iota(shape, axis):
    return lax.broadcasted_iota(jnp.int32, shape, axis)


def column(row):
    n = row.shape[1]
    eye = iota((n, n), 0) == iota((n, n), 1)
    return jnp.sum(jnp.where(eye, row, jnp.zeros_like(row)), axis=1, keepdims=True)


def as_row(col):
    n = col.shape[0]
    eye = iota((n, n), 0) == iota((n, n), 1)
    return jnp.sum(jnp.where(eye, col, jnp.zeros_like(col)), axis=0, keepdims=True)


def destinations(routes_ref, experts, capacity):
    tok = routes_ref.shape[1]
    first, second = routes_ref[0:1, :], routes_ref[1:2, :]
    ids = iota((experts, tok), 0)
    hot0 = (ids == first).astype(F32)
    hot1 = (ids == second).astype(F32)
    before = (iota((tok, tok), 0) < iota((tok, tok), 1)).astype(F32).astype(BF16)
    count0 = jnp.dot(hot0.astype(BF16), before, preferred_element_type=F32)
    count1 = jnp.dot(hot1.astype(BF16), before, preferred_element_type=F32)
    count1 = count1 + jnp.sum(hot0, axis=1, keepdims=True)
    pos0 = jnp.sum(hot0 * count0, axis=0, keepdims=True)
    pos1 = jnp.sum(hot1 * count1, axis=0, keepdims=True)
    return (
        first * capacity + pos0.astype(jnp.int32),
        second * capacity + pos1.astype(jnp.int32),
    )


def pack_kernel(experts, capacity, routes_ref, gates_ref, tokens_ref, cot_ref, out_ref):
    slots = experts * capacity
    tok, width = tokens_ref.shape
    dest0, dest1 = destinations(routes_ref, experts, capacity)
    rows = iota((slots, tok), 0)
    pick = jnp.concatenate(
        [(rows == dest0).astype(F32).astype(BF16), (rows == dest1).astype(F32).astype(BF16)],
        axis=1,
    )
    cot = cot_ref[...].astype(F32)
    grad0 = (column(gates_ref[0:1, :]) * cot).astype(BF16)
    grad1 = (column(gates_ref[1:2, :]) * cot).astype(BF16)
    tokens = tokens_ref[...]
    out_ref[:, :width] = jnp.dot(
        pick, jnp.concatenate([tokens, tokens], axis=0), preferred_element_type=F32
    ).astype(BF16)
    out_ref[:, width:] = jnp.dot(
        pick, jnp.concatenate([grad0, grad1], axis=0), preferred_element_type=F32
    ).astype(BF16)


def combine_kernel(
    experts, capacity, routes_ref, gates_ref, cot_ref, ret_ref, out_ref, tgrad_ref, ggrad_ref
):
    slots = experts * capacity
    tok, width = cot_ref.shape
    dest0, dest1 = destinations(routes_ref, experts, capacity)
    cols = iota((tok, slots), 1)
    dest0 = column(dest0.astype(F32)).astype(jnp.int32)
    dest1 = column(dest1.astype(F32)).astype(jnp.int32)
    pick = jnp.concatenate(
        [(cols == dest0).astype(F32).astype(BF16), (cols == dest1).astype(F32).astype(BF16)],
        axis=0,
    )
    slot_out = jnp.dot(pick, ret_ref[:, :width], preferred_element_type=F32)
    slot_grad = jnp.dot(pick, ret_ref[:, width:], preferred_element_type=F32)
    out0, out1 = slot_out[:tok], slot_out[tok:]
    gate0, gate1 = column(gates_ref[0:1, :]), column(gates_ref[1:2, :])
    out_ref[...] = (gate0 * out0 + gate1 * out1).astype(BF16)
    tgrad_ref[...] = (slot_grad[:tok] + slot_grad[tok:]).astype(BF16)
    cot = cot_ref[...].astype(F32)
    ggrad_ref[0:1, :] = as_row(jnp.sum(cot * out0, axis=1, keepdims=True))
    ggrad_ref[1:2, :] = as_row(jnp.sum(cot * out1, axis=1, keepdims=True))


def expert_kernel(chunk, rows_ref, w1_ref, w2_ref, ret_ref, hidden_ref, pgrad_ref):
    width = w1_ref.shape[0]
    inner = w1_ref.shape[1]
    x = rows_ref[:, :width]
    g = rows_ref[:, width:]
    for start in range(0, inner, chunk):
        part = slice(start, start + chunk)
        v = jnp.dot(x, w1_ref[:, part], preferred_element_type=F32)
        hgrad = lax.dot_general(g, w2_ref[part, :], NT, preferred_element_type=F32)
        sq = v * v
        half = 0.5 + 0.5 * jnp.tanh(v * (tanh_scale + (tanh_scale * cubic_term) * sq))
        hidden = v * half
        slope = half + hidden * (1.0 - half) * (
            2.0 * tanh_scale + (6.0 * tanh_scale * cubic_term) * sq
        )
        hidden_ref[:, part] = hidden.astype(BF16)
        pgrad_ref[:, part] = (hgrad * slope).astype(BF16)
    ret_ref[:, :width] = jnp.dot(
        hidden_ref[...], w2_ref[...], preferred_element_type=F32
    ).astype(BF16)
    ret_ref[:, width:] = lax.dot_general(
        pgrad_ref[...], w1_ref[...], NT, preferred_element_type=F32
    ).astype(BF16)


def weight_kernel(n, place_ref, *refs):
    pieces, right_ref = refs[:n], refs[n]
    outs = refs[n + 1 : 2 * n + 1]
    left_ref = refs[2 * n + 1]
    part = pieces[0].shape[1]

    @pl.when(pl.program_id(0) == 0)
    def _():
        for d in range(n):
            left_ref[d * part : (d + 1) * part, :] = pieces[d][...].T

    product = jnp.dot(left_ref[...], right_ref[...], preferred_element_type=F32).astype(BF16)
    for d in range(n):
        outs[d][...] = product[d * part : (d + 1) * part]


def sum_kernel(n, flip, *refs):
    total = refs[0][...].astype(F32)
    for d in range(1, n):
        total = total + refs[d][...].astype(F32)
    refs[n][...] = total.T if flip else total


def params():
    return pltpu.CompilerParams(vmem_limit_bytes=VMEM_LIMIT)


def shards(tokens, routes, gate_weights, cotangent, expand_weight, reduce_weight):
    tok, width = tokens.shape
    experts = lax.axis_size("expert")
    n_dp = lax.axis_size("dp")
    capacity = 8 * tok // experts
    slots = experts * capacity
    w1, w2 = expand_weight[0], reduce_weight[0]
    inner = w1.shape[1]
    routes_t, gates_t = routes.T, gate_weights.T
    part = width // n_dp

    packed = pl.pallas_call(
        functools.partial(pack_kernel, experts, capacity),
        out_shape=jax.ShapeDtypeStruct((slots, 2 * width), BF16),
        compiler_params=params(),
        name="pack",
    )(routes_t, gates_t, tokens, cotangent)
    arrived = lax.all_to_all(
        packed.reshape(experts, capacity, 2 * width), "expert", 0, 0, tiled=True
    ).reshape(slots, 2 * width)

    tile = 256
    once = pl.Buffered(1)
    ret, hidden, pgrad = pl.pallas_call(
        functools.partial(expert_kernel, 512),
        grid=(slots // tile,),
        in_specs=[
            pl.BlockSpec((tile, 2 * width), lambda i: (i, 0)),
            pl.BlockSpec(memory_space=pltpu.VMEM),
            pl.BlockSpec(memory_space=pltpu.VMEM),
        ],
        out_specs=[
            pl.BlockSpec((tile, 2 * width), lambda i: (i, 0)),
            pl.BlockSpec((tile, inner), lambda i: (i, 0)),
            pl.BlockSpec((tile, inner), lambda i: (i, 0)),
        ],
        out_shape=[
            jax.ShapeDtypeStruct((slots, 2 * width), BF16),
            jax.ShapeDtypeStruct((slots, inner), BF16),
            jax.ShapeDtypeStruct((slots, inner), BF16),
        ],
        compiler_params=params(),
        cost_estimate=pl.CostEstimate(
            flops=8 * slots * width * inner, bytes_accessed=16 << 20, transcendentals=0
        ),
        name="expert",
    )(arrived, w1, w2)
    returned = lax.all_to_all(
        ret.reshape(experts, capacity, 2 * width), "expert", 0, 0, tiled=True
    ).reshape(slots, 2 * width)

    place = lax.axis_index("dp").astype(jnp.int32).reshape(1)
    htile = 512

    def piece(d, base):
        return pl.BlockSpec(
            (slots, part),
            lambda i, p: (0, base + lax.rem(p[0] + d, n_dp)),
            pipeline_mode=once,
        )

    def weight_grad(base, right):
        pieces = pl.pallas_call(
            functools.partial(weight_kernel, n_dp),
            grid_spec=pltpu.PrefetchScalarGridSpec(
                num_scalar_prefetch=1,
                grid=(inner // htile,),
                in_specs=[piece(d, base) for d in range(n_dp)]
                + [pl.BlockSpec((slots, htile), lambda i, p: (0, i))],
                out_specs=[pl.BlockSpec((part, htile), lambda i, p: (0, i))] * n_dp,
                scratch_shapes=[pltpu.VMEM((width, slots), BF16)],
            ),
            out_shape=[jax.ShapeDtypeStruct((part, inner), BF16)] * n_dp,
            compiler_params=params(),
            cost_estimate=pl.CostEstimate(
                flops=2 * slots * width * inner, bytes_accessed=7 << 20, transcendentals=0
            ),
        )(place, *([arrived] * n_dp), right)
        return [pieces[0]] + [
            lax.ppermute(pieces[d], "dp", [(i, (i + d) % n_dp) for i in range(n_dp)])
            for d in range(1, n_dp)
        ]

    def total(parts, flip):
        spec = pl.BlockSpec((part, htile), lambda i: (0, i))
        flipped = pl.BlockSpec((htile, part), lambda i: (i, 0))
        shape = (inner, part) if flip else (part, inner)
        return pl.pallas_call(
            functools.partial(sum_kernel, n_dp, flip),
            grid=(inner // htile,),
            in_specs=[spec] * n_dp,
            out_specs=flipped if flip else spec,
            out_shape=jax.ShapeDtypeStruct(shape, F32),
            compiler_params=params(),
            cost_estimate=pl.CostEstimate(
                flops=1 << 20, bytes_accessed=3 << 20, transcendentals=0
            ),
        )(*parts)

    reduce_parts = weight_grad(n_dp, hidden)
    expand_parts = weight_grad(0, pgrad)
    reduce_grad = total(reduce_parts, True)
    layer_out, token_grad, gate_grad = pl.pallas_call(
        functools.partial(combine_kernel, experts, capacity),
        in_specs=[pl.BlockSpec(memory_space=pltpu.VMEM)] * 4,
        out_shape=[
            jax.ShapeDtypeStruct((tok, width), BF16),
            jax.ShapeDtypeStruct((tok, width), BF16),
            jax.ShapeDtypeStruct((2, tok), F32),
        ],
        compiler_params=params(),
        cost_estimate=pl.CostEstimate(
            flops=8 * slots * tok * width, bytes_accessed=3 << 20, transcendentals=0
        ),
        name="combine",
    )(routes_t, gates_t, cotangent, returned)
    expand_grad = total(expand_parts, False)
    return (layer_out, token_grad, gate_grad.T, expand_grad[None], reduce_grad[None])


def solution(mesh):
    return jax.shard_map(
        shards,
        mesh=mesh,
        in_specs=(
            P(("expert", "dp"), None),
            P(("expert", "dp"), None),
            P(("expert", "dp"), None),
            P(("expert", "dp"), None),
            P("expert", None, None),
            P("expert", None, None),
        ),
        out_specs=(
            P(("expert", "dp"), None),
            P(("expert", "dp"), None),
            P(("expert", "dp"), None),
            P("expert", "dp", None),
            P("expert", None, "dp"),
        ),
        check_vma=False,
    )
```
